256 devices in a mesh: sub: 16 (over z, core), root: 16 (over y, x).
Axes of the slice: x: 4, y: 4, z: 8, core: 2. Of those that a mesh axis runs over, the one named last changes fastest.
Arguments:
- right_side: bfloat16 [16, 32768, 256], P('root', 'sub'), may hold values from -6 to 6
- leaf_inverse: bfloat16 [16, 32768, 512], P('root', 'sub'), may hold values from -0.25 to 0.25
- leaf_basis: bfloat16 [16, 32768, 256], P('root', 'sub'), may hold values from -0.25 to 0.25
- local_merge: bfloat16 [16, 24576, 512], P('root', 'sub'), may hold values from -0.25 to 0.25
- local_transfer: bfloat16 [16, 24576, 256], P('root', 'sub'), may hold values from -0.25 to 0.25
- upper_merge: bfloat16 [16, 7680, 512], P('root', 'sub'), may hold values from -0.25 to 0.25
- upper_transfer: bfloat16 [16, 7680, 256], P('root', 'sub'), may hold values from -0.25 to 0.25
- top_inverse: bfloat16 [4096, 4096], P('root', 'sub'), may hold values from -0.09375 to 0.09375
Outputs:
- solution: float32 [16, 32768, 256], P('root', 'sub')
The draws below stay inside these ranges and needn't reach their ends.
All inputs are finite; a program needn't handle non-finite values.
Results may differ from the reference program's by a relative error of at most 0.02.
Values may be sent and summed in bfloat16 or wider, within the bound.
A program may use at most 128 MiB of HBM per device.

```python
import jax
import jax.numpy as jnp
from jax import lax

LEAF = 512
RANK = 256
NRHS = 256
LEAVES_DEV = 4
LOG_LEAF = 2
LOG_SUB = 4
UPPER_ROWS = 480
TOP_ORDER = 4096
N_SUB = 16
N_ROOT = 16


def block_scale(key, dims, split, low, high):
    gain = 1.0
    for axis_at, shards_of in split:
        steps = jax.random.uniform(jax.random.fold_in(jax.random.fold_in(key, 6), axis_at), (shards_of,), jnp.float32, low / len(split), high / len(split))
        gain = gain * jnp.repeat(jnp.exp(steps), dims[axis_at] // shards_of).reshape((-1,) + (1,) * (len(dims) - 1 - axis_at))
    return gain


def centred(stream_key, shape, width, limit, shards=(), kind=jnp.bfloat16):
    gain = block_scale(stream_key, shape, shards, -0.22, 0.18) if shards else 1.0
    array = jax.random.normal(stream_key, shape, jnp.float32) * width * gain
    return jnp.minimum(jnp.maximum(array, -limit), limit).astype(kind)


def setup_inputs(seed: int = 0) -> dict:
    keys = jax.random.split(jax.random.key(seed), 9)
    return {
        "right_side": centred(keys[0], (N_ROOT, N_SUB * LEAVES_DEV * LEAF, NRHS), 1.0, 6.0, ((0, 16), (1, 16))),
        "leaf_inverse": centred(keys[1], (N_ROOT, N_SUB * LEAVES_DEV * LEAF, LEAF), LEAF ** -0.5, 0.25, ((0, 16), (1, 16))),
        "leaf_basis": centred(keys[2], (N_ROOT, N_SUB * LEAVES_DEV * LEAF, RANK), LEAF ** -0.5, 0.25, ((0, 16), (1, 16))),
        "local_merge": centred(keys[3], (N_ROOT, N_SUB * (LEAVES_DEV - 1) * 2 * RANK, 2 * RANK), (2 * RANK) ** -0.5, 0.25, ((0, 16), (1, 16))),
        "local_transfer": centred(keys[4], (N_ROOT, N_SUB * (LEAVES_DEV - 1) * 2 * RANK, RANK), (2 * RANK) ** -0.5, 0.25, ((0, 16), (1, 16))),
        "upper_merge": centred(keys[5], (N_ROOT, N_SUB * UPPER_ROWS, 2 * RANK), (2 * RANK) ** -0.5, 0.25, ((0, 16), (1, 16))),
        "upper_transfer": centred(keys[6], (N_ROOT, N_SUB * UPPER_ROWS, RANK), (2 * RANK) ** -0.5, 0.25, ((0, 16), (1, 16))),
        "top_inverse": centred(keys[7], (TOP_ORDER, TOP_ORDER), TOP_ORDER ** -0.5, 0.09375, ((0, 16), (1, 16))),
    }


def batch_product(left, right):
    return jnp.einsum("nij,njk->nik", left.astype(jnp.float32), right.astype(jnp.float32))


def batch_transposed(left, right):
    return jnp.einsum("nji,njk->nik", left.astype(jnp.float32), right.astype(jnp.float32))


def merge_up(coeffs, merge_mat, transfer):
    paired = coeffs.astype(jnp.bfloat16).reshape(merge_mat.shape[0], 2 * RANK, NRHS)
    inner_part = batch_product(merge_mat, paired)
    parent = batch_transposed(transfer, inner_part.astype(jnp.bfloat16))
    return inner_part, parent


def merge_down(parent, inner_part, merge_mat, transfer):
    lifted = batch_product(transfer, parent.astype(jnp.bfloat16)).astype(jnp.bfloat16)
    children = inner_part - batch_product(merge_mat, lifted)
    return children.reshape(-1, RANK, NRHS)


def local_level(block, tier_no):
    node_count = LEAVES_DEV >> tier_no
    start = LEAVES_DEV - 2 * node_count
    shaped = block.reshape(N_SUB, LEAVES_DEV - 1, 2 * RANK, block.shape[-1])
    return shaped[:, start:start + node_count].reshape(N_SUB * node_count, 2 * RANK, block.shape[-1])


def upper_level(block, tier_no):
    height = (2 * RANK) >> tier_no
    offset = 2 * RANK - 2 * height
    shaped = block.reshape(N_SUB, block.shape[0] // N_SUB, block.shape[-1])
    return shaped[:, offset:offset + height].reshape(N_SUB >> tier_no, 2 * RANK, block.shape[-1])


def climb(operands):
    right_side, leaf_inv, basis_block, local_m, local_w, upper_m, upper_w = operands
    leaves = N_SUB * LEAVES_DEV
    solved = batch_product(leaf_inv.reshape(leaves, LEAF, LEAF), right_side.reshape(leaves, LEAF, NRHS))
    coeffs = batch_transposed(basis_block.reshape(leaves, LEAF, RANK), solved.astype(jnp.bfloat16))
    inner_saved = []
    for tier_no in range(1, LOG_LEAF + 1):
        inner_part, coeffs = merge_up(coeffs, local_level(local_m, tier_no), local_level(local_w, tier_no))
        inner_saved.append(inner_part)
    for tier_no in range(1, LOG_SUB + 1):
        inner_part, coeffs = merge_up(coeffs, upper_level(upper_m, tier_no), upper_level(upper_w, tier_no))
        inner_saved.append(inner_part)
    return solved, tuple(inner_saved), coeffs[0].astype(jnp.bfloat16)


def descend(operands):
    coupling, solved, inner_saved, leaf_inv, basis_block, local_m, local_w, upper_m, upper_w = operands
    leaves = N_SUB * LEAVES_DEV
    parent = coupling[None]
    for tier_no in range(LOG_SUB, 0, -1):
        parent = merge_down(parent, inner_saved[LOG_LEAF + tier_no - 1], upper_level(upper_m, tier_no), upper_level(upper_w, tier_no))
    for tier_no in range(LOG_LEAF, 0, -1):
        parent = merge_down(parent, inner_saved[tier_no - 1], local_level(local_m, tier_no), local_level(local_w, tier_no))
    spread = batch_product(basis_block.reshape(leaves, LEAF, RANK), parent.astype(jnp.bfloat16)).astype(jnp.bfloat16)
    result = solved - batch_product(leaf_inv.reshape(leaves, LEAF, LEAF), spread)
    return result.reshape(leaves * LEAF, NRHS)


def reference(right_side, leaf_inverse, leaf_basis, local_merge, local_transfer, upper_merge, upper_transfer, top_inverse):
    solved, inner_saved, roots = lax.map(climb, (right_side, leaf_inverse, leaf_basis, local_merge, local_transfer, upper_merge, upper_transfer))
    stacked = roots.reshape(N_ROOT * RANK, NRHS)
    coupling = jnp.dot(top_inverse, stacked, preferred_element_type=jnp.float32).reshape(N_ROOT, RANK, NRHS)
    return lax.map(descend, (coupling, solved, inner_saved, leaf_inverse, leaf_basis, local_merge, local_transfer, upper_merge, upper_transfer))
```

```python
import jax
import jax.numpy as jnp
from jax import lax
from jax.experimental import pallas as pl
from jax.experimental.pallas import tpu as pltpu
from jax.sharding import PartitionSpec as P

MESH = pl.DeviceIdType.MESH
BF = jnp.bfloat16
F32 = jnp.float32


def mul(a, b):
    return lax.dot_general(a, b, (((1,), (0,)), ((), ())), preferred_element_type=F32)


def mul_t(a, b):
    return lax.dot_general(a, b, (((1,), (1,)), ((), ())), preferred_element_type=F32)


def t_mul(a, b):
    return lax.dot_general(a, b, (((0,), (0,)), ((), ())), preferred_element_type=F32)


def kernel(
    b_hbm, d_hbm, u_hbm, lm_hbm, lw_hbm, um_hbm, uw_hbm, top_hbm,
    out_hbm,
    bv, dv, uv, lm, lw, m1, w1, m2, w2, rm, rw, tp,
    cl, cn, ct, p1, c1, p2, c2, p34, rt, t4,
    t2s, f2, t1s, f1, t0s, f0, gq, sv, hv,
    load_sem, own_sem, out_sem, send_sem, up_sem, ring_sem, small_sem, root_sem, t4_sem,
):
    s = lax.axis_index("sub")
    r = lax.axis_index("root")
    k = lax.rem(s, 2)
    z0 = lax.rem(s // 2, 2)
    g = s // 4
    slot = 8 * k + 4 * z0 + g
    partner = s + 1 - 2 * k
    across = s + 2 - 4 * z0
    right = lax.rem(s + 2, 16)
    left = lax.rem(s + 14, 16)

    barrier = pltpu.get_barrier_semaphore()
    for i in range(1, 16):
        pl.semaphore_signal(barrier, inc=1, device_id=(lax.rem(s + i, 16), r), device_id_type=MESH)
    for i in range(1, 16):
        pl.semaphore_signal(barrier, inc=1, device_id=(s, lax.rem(r + i, 16)), device_id_type=MESH)

    def load(i):
        rows = pl.ds(i * 512, 512)
        return [
            pltpu.make_async_copy(d_hbm.at[rows], dv.at[i], load_sem.at[0, i]),
            pltpu.make_async_copy(b_hbm.at[rows], bv.at[i], load_sem.at[1, i]),
            pltpu.make_async_copy(u_hbm.at[rows], uv.at[i], load_sem.at[2, i]),
        ]

    def load_local(i):
        rows = pl.ds(i * 512, 512)
        return [
            pltpu.make_async_copy(lm_hbm.at[rows], lm.at[i], load_sem.at[3, i]),
            pltpu.make_async_copy(lw_hbm.at[rows], lw.at[i], load_sem.at[4, i]),
        ]

    for i in range(4):
        for c in load(i):
            c.start()
    for i in range(3):
        for c in load_local(i):
            c.start()
    place1 = pl.ds(k * 256, 256)
    place2 = 2 * z0 + k
    here2 = pl.ds(place2 * 128, 128)
    first, second, third = pl.ds(0, 256), pl.ds(256, 128), pl.ds(384, 96)
    own = [
        pltpu.make_async_copy(um_hbm.at[first], m1.at[place1], own_sem.at[0]),
        pltpu.make_async_copy(uw_hbm.at[first], w1.at[place1], own_sem.at[1]),
        pltpu.make_async_copy(um_hbm.at[second], m2.at[here2], own_sem.at[2]),
        pltpu.make_async_copy(uw_hbm.at[second], w2.at[here2], own_sem.at[3]),
        pltpu.make_async_copy(um_hbm.at[third], rm.at[s], own_sem.at[4]),
        pltpu.make_async_copy(uw_hbm.at[third], rw.at[s], own_sem.at[5]),
        pltpu.make_async_copy(top_hbm, tp.at[s], own_sem.at[6]),
    ]
    for c in own:
        c.start()

    sent = []

    def send(src, dst, sem, to):
        copy = pltpu.make_async_remote_copy(
            src_ref=src, dst_ref=dst, send_sem=send_sem.at[len(sent)], recv_sem=sem,
            device_id=to, device_id_type=MESH,
        )
        copy.start()
        sent.append(copy)

    def arrived(dst, sem):
        pltpu.make_async_remote_copy(
            src_ref=dst, dst_ref=dst, send_sem=send_sem.at[0], recv_sem=sem,
            device_id=(partner, r), device_id_type=MESH,
        ).wait_recv()

    pl.semaphore_wait(barrier, 30)

    rings = ((um_hbm.at[third], rm), (uw_hbm.at[third], rw), (top_hbm, tp))

    def ring_own(a):
        src, dst = rings[a]
        send(src, dst.at[s], ring_sem.at[a, s], (right, r))
        send(src, dst.at[s], ring_sem.at[a, s], (left, r))
        send(src, dst.at[s], ring_sem.at[a, s], (partner, r))

    reach = ((4, 3), (3, 4), (3, 4))

    def relay(a, hop):
        dst = rings[a][1]
        if hop <= reach[a][0]:
            b = lax.rem(s + 16 - 2 * hop, 16)
            arrived(dst.at[b], ring_sem.at[a, b])
            if hop < reach[a][0]:
                send(dst.at[b], dst.at[b], ring_sem.at[a, b], (right, r))
            send(dst.at[b], dst.at[b], ring_sem.at[a, b], (partner, r))
        if hop <= reach[a][1]:
            b = lax.rem(s + 2 * hop, 16)
            arrived(dst.at[b], ring_sem.at[a, b])
            if hop < reach[a][1]:
                send(dst.at[b], dst.at[b], ring_sem.at[a, b], (left, r))
            send(dst.at[b], dst.at[b], ring_sem.at[a, b], (partner, r))

    def ring_rest(a):
        dst = rings[a][1]
        for i in range(8):
            b = lax.rem(partner + 2 * i, 16)
            arrived(dst.at[b], ring_sem.at[a, b])

    ring_own(0)
    ring_own(1)
    send(um_hbm.at[second], m2.at[here2], up_sem.at[0, place2], (across, r))
    send(uw_hbm.at[second], w2.at[here2], up_sem.at[1, place2], (across, r))
    send(um_hbm.at[first], m1.at[place1], up_sem.at[2, k], (partner, r))
    send(uw_hbm.at[first], w1.at[place1], up_sem.at[3, k], (partner, r))
    send(um_hbm.at[second], m2.at[here2], up_sem.at[0, place2], (partner, r))
    send(uw_hbm.at[second], w2.at[here2], up_sem.at[1, place2], (partner, r))

    def leaf_up(i, carry):
        for c in load(i):
            c.wait()
        solved = mul(dv[i], bv[i]).astype(BF)
        cl[i] = t_mul(solved, uv[i]).astype(BF)
        return carry

    lax.fori_loop(0, 4, leaf_up, 0)

    def node_up(pair, m, w):
        inner = mul_t(pair, m).astype(BF)
        return mul(inner, w).astype(BF)

    def local_up(i, carry):
        for c in load_local(i):
            c.wait()
        cn[i] = node_up(jnp.concatenate([cl[2 * i], cl[2 * i + 1]], axis=1), lm[i], lw[i])
        return carry

    lax.fori_loop(0, 2, local_up, 0)
    for c in load_local(2):
        c.wait()
    ct[...] = node_up(jnp.concatenate([cn[0], cn[1]], axis=1), lm[2], lw[2])

    send(ct.at[pl.ds(128 - 128 * k, 128)], p1.at[k], small_sem.at[0], (partner, r))
    p1[k] = ct[pl.ds(pl.multiple_of(128 * k, 128), 128), :]
    for c in own[:4]:
        c.wait()
    arrived(m1.at[pl.ds(256 - k * 256, 256)], up_sem.at[2, 1 - k])
    arrived(w1.at[pl.ds(256 - k * 256, 256)], up_sem.at[3, 1 - k])
    arrived(p1.at[1 - k], small_sem.at[0])
    c1[...] = node_up(jnp.concatenate([p1[0], p1[1]], axis=1), m1[...], w1[...])

    send(c1.at[pl.ds(64 - 64 * z0, 64)], p2.at[z0], small_sem.at[1], (across, r))
    p2[z0] = c1[pl.ds(pl.multiple_of(64 * z0, 64), 64), :]
    there2 = 2 - 2 * z0 + k
    there2_rows = pl.ds(there2 * 128, 128)
    arrived(m2.at[there2_rows], up_sem.at[0, there2])
    send(m2.at[there2_rows], m2.at[there2_rows], up_sem.at[0, there2], (partner, r))
    arrived(w2.at[there2_rows], up_sem.at[1, there2])
    send(w2.at[there2_rows], w2.at[there2_rows], up_sem.at[1, there2], (partner, r))
    relay(0, 1)
    relay(1, 1)
    ring_own(2)
    for c in (2 * z0 + 1 - k, 2 - 2 * z0 + 1 - k):
        rows = pl.ds(c * 128, 128)
        arrived(m2.at[rows], up_sem.at[0, c])
        arrived(w2.at[rows], up_sem.at[1, c])
    arrived(p2.at[1 - z0], small_sem.at[1])
    c2[...] = node_up(
        jnp.concatenate([p2[0], p2[1]], axis=1), m2[...], w2[...]
    ).reshape(4, 16, 256)

    for i in range(1, 4):
        h = lax.rem(g + i, 4)
        send(c2.at[h], p34.at[g], small_sem.at[2 + g], (4 * h + lax.rem(s, 4), r))
    p34[g] = c2[g]
    relay(0, 2)
    relay(1, 2)
    relay(2, 1)
    relay(0, 3)
    relay(1, 3)
    relay(0, 4)
    relay(1, 4)
    own[4].wait()
    own[5].wait()
    ring_rest(0)
    ring_rest(1)
    for i in range(1, 4):
        h = lax.rem(g + i, 4)
        arrived(p34.at[h], small_sem.at[2 + h])

    def m3(n):
        return rm[8 * n : 8 * n + 8, 0:64, :].reshape(512, 512)

    def w3(n):
        return rw[8 * n : 8 * n + 8, 0:64, :].reshape(512, 256)

    def m4():
        return rm[:, 64:96, :].reshape(512, 512)

    def w4():
        return rw[:, 64:96, :].reshape(512, 256)

    pairs = [jnp.concatenate([p34[2 * n], p34[2 * n + 1]], axis=1) for n in range(2)]
    c3 = [node_up(pairs[n], m3(n), w3(n)) for n in range(2)]
    inner4 = mul_t(jnp.concatenate(c3, axis=1), m4()).astype(BF)
    rt[r] = mul(inner4, w4()).astype(BF)

    for i in range(1, 16):
        send(rt.at[r], rt.at[r], root_sem.at[r], (s, lax.rem(r + i, 16)))

    for n in range(2):
        x = (pairs[n].astype(F32) - mul_t(inner4[:, 256 * n : 256 * n + 256], w3(n))).astype(BF)
        t2 = mul_t(x, m3(n)).astype(BF)
        t2s[2 * n] = t2[:, :256]
        t2s[2 * n + 1] = t2[:, 256:]
    for i in range(1, 4):
        h = lax.rem(g + i, 4)
        send(t2s.at[h], f2.at[g], small_sem.at[6 + g], (4 * h + lax.rem(s, 4), r))
    f2[g] = t2s[g]
    relay(2, 2)

    n_up = s // 8
    m4h = rm[pl.ds(8 * n_up, 8), 64:96, :].reshape(256, 512)
    e = mul(m4h, w4()).astype(BF)
    m3h = rm[pl.ds(4 * g, 4), 0:64, :].reshape(256, 512)
    w3h = rw[pl.ds(8 * n_up, 8), 0:64, :].reshape(512, 256)
    e = mul(m3h, mul(w3h, e).astype(BF)).astype(BF)
    m2h = m2[pl.ds(pl.multiple_of(256 * z0, 256), 256), :]
    e = mul(m2h, mul(w2[...], e).astype(BF)).astype(BF)
    m1h = m1[pl.ds(pl.multiple_of(256 * k, 256), 256), :]
    gq[...] = mul(m1h, mul(w1[...], e).astype(BF)).astype(BF)
    relay(2, 3)
    relay(2, 4)
    own[6].wait()
    ring_rest(2)

    for i in range(1, 16):
        q = lax.rem(r + i, 16)
        arrived(rt.at[q], root_sem.at[q])
    total = mul_t(rt[0], tp[0])
    for q in range(1, 16):
        total += mul_t(rt[q], tp[q])
    t4[slot] = total.astype(BF)
    for i in range(1, 16):
        send(t4.at[slot], t4.at[slot], t4_sem.at[slot], (lax.rem(s + i, 16), r))

    for i in range(1, 4):
        h = lax.rem(g + i, 4)
        arrived(f2.at[h], small_sem.at[6 + h])

    def node_down(pair, t, m, w):
        x = (pair.astype(F32) - mul_t(t, w)).astype(BF)
        return mul_t(x, m).astype(BF)

    t1 = node_down(
        jnp.concatenate([p2[0], p2[1]], axis=1), f2[...].reshape(64, 256), m2[...], w2[...]
    )
    t1s[0] = t1[:, :256]
    t1s[1] = t1[:, 256:]
    send(t1s.at[1 - z0], f1.at[z0], small_sem.at[10], (across, r))
    f1[z0] = t1s[z0]
    lo = mul(lm[2], mul(lw[2], gq[...]).astype(BF)).astype(BF)

    def down_gain(n, gain):
        e2 = mul(lm[n], mul(lw[n], gain).astype(BF)).astype(BF)
        for j in range(2):
            i = 2 * n + j
            ue = mul(uv[i], e2[256 * j : 256 * j + 256, :]).astype(BF)
            hv[i] = mul(dv[i], ue).astype(BF)

    down_gain(0, lo[:256])
    arrived(f1.at[1 - z0], small_sem.at[10])
    t0 = node_down(
        jnp.concatenate([p1[0], p1[1]], axis=1), f1[...].reshape(128, 256), m1[...], w1[...]
    )
    t0s[0] = t0[:, :256]
    t0s[1] = t0[:, 256:]
    send(t0s.at[1 - k], f0.at[k], small_sem.at[11], (partner, r))
    f0[k] = t0s[k]
    down_gain(1, lo[256:])
    arrived(f0.at[1 - k], small_sem.at[11])
    ta = node_down(
        jnp.concatenate([cn[0], cn[1]], axis=1), f0[...].reshape(256, 256), lm[2], lw[2]
    )
    for n in range(2):
        tb = node_down(
            jnp.concatenate([cl[2 * n], cl[2 * n + 1]], axis=1),
            ta[:, 256 * n : 256 * n + 256], lm[n], lw[n],
        )
        for j in range(2):
            i = 2 * n + j
            x = (bv[i].astype(F32) - mul_t(uv[i], tb[:, 256 * j : 256 * j + 256])).astype(BF)
            sv[i] = mul(dv[i], x)

    for i in range(1, 16):
        q = lax.rem(s + i, 16)
        q = 8 * lax.rem(q, 2) + 4 * lax.rem(q // 2, 2) + q // 4
        arrived(t4.at[q], t4_sem.at[q])
    top = t4[...].reshape(256, 256)

    def last(i):
        return pltpu.make_async_copy(sv.at[i], out_hbm.at[pl.ds(i * 512, 512)], out_sem.at[i])

    def finish(i, carry):
        sv[i] = sv[i] - mul_t(hv[i], top)
        last(i).start()
        return carry

    lax.fori_loop(0, 4, finish, 0)
    for copy in sent:
        copy.wait_send()
    for i in range(4):
        last(i).wait()


def body(b, d, u, lm, lw, um, uw, top):
    flat = [a.reshape(a.shape[-2:]) for a in (b, d, u, lm, lw, um, uw, top)]
    dma = pltpu.SemaphoreType.DMA
    vm = pltpu.VMEM
    out = pl.pallas_call(
        kernel,
        out_shape=jax.ShapeDtypeStruct((2048, 256), F32),
        in_specs=[pl.BlockSpec(memory_space=pl.ANY)] * 8,
        out_specs=pl.BlockSpec(memory_space=pl.ANY),
        scratch_shapes=[
            vm((4, 512, 256), BF), vm((4, 512, 512), BF), vm((4, 512, 256), BF),
            vm((3, 512, 512), BF), vm((3, 512, 256), BF),
            vm((512, 512), BF), vm((512, 256), BF), vm((512, 512), BF), vm((512, 256), BF),
            vm((16, 96, 512), BF), vm((16, 96, 256), BF), vm((16, 256, 256), BF),
            vm((4, 256, 256), BF), vm((2, 256, 256), BF), vm((256, 256), BF),
            vm((2, 128, 256), BF), vm((128, 256), BF), vm((2, 64, 256), BF), vm((4, 16, 256), BF),
            vm((4, 16, 256), BF), vm((16, 16, 256), BF), vm((16, 16, 256), BF),
            vm((4, 16, 256), BF), vm((4, 16, 256), BF), vm((2, 64, 256), BF), vm((2, 64, 256), BF),
            vm((2, 128, 256), BF), vm((2, 128, 256), BF), vm((256, 256), BF),
            vm((4, 512, 256), F32), vm((4, 512, 256), BF),
            dma((5, 4)), dma((7,)), dma((4,)), dma((104,)), dma((4, 4)), dma((3, 16)),
            dma((12,)), dma((16,)), dma((16,)),
        ],
        compiler_params=pltpu.CompilerParams(
            collective_id=0, has_side_effects=True, vmem_limit_bytes=56 << 20
        ),
    )(*flat)
    return out.reshape(1, 2048, 256)


def solution(mesh):
    rows = P("root", "sub", None)
    return jax.shard_map(
        body, mesh=mesh, in_specs=(rows,) * 7 + (P("root", "sub"),), out_specs=rows, check_vma=False
    )
```

```python
import jax
import jax.numpy as jnp
from jax import lax
from jax.experimental import pallas as pl
from jax.experimental.pallas import tpu as pltpu
from jax.sharding import PartitionSpec as P

MESH = pl.DeviceIdType.MESH
BF = jnp.bfloat16
F32 = jnp.float32


def mul(a, b):
    return lax.dot_general(a, b, (((1,), (0,)), ((), ())), preferred_element_type=F32)


def mul_t(a, b):
    return lax.dot_general(a, b, (((1,), (1,)), ((), ())), preferred_element_type=F32)


def t_mul(a, b):
    return lax.dot_general(a, b, (((0,), (0,)), ((), ())), preferred_element_type=F32)


class V:
    def __init__(self, ref, index=None):
        self.ref, self.index = ref, index

    def __getitem__(self, index):
        return V(self.ref, index)


def at(view):
    return view.ref.at[view.index] if isinstance(view, V) else view


def kernel(
    b_hbm, d_hbm, u_hbm, lm_hbm, lw_hbm, um_hbm, uw_hbm, top_hbm,
    out_hbm,
    bv, dv, uv, lm, lw, m1, w1, m2, w2, rm, rw, xm, xw, tp,
    cl, cn, ct, p1, p2, c1, c2, p3, p4, rt, t4,
    t2s, f2, t1s, f1, t0s, f0, ks, kr, sv, hv,
    load_sem, own_sem, out_sem, both_sem, proc_sem, edge_sem, root_send_sem,
    up_sem, ring_sem, small_sem, root_sem, t4_sem,
):
    s = lax.axis_index("sub")
    r = lax.axis_index("root")
    k = lax.rem(s, 2)
    q = lax.rem(s // 2, 4)
    is_proc = lax.rem((q + 1) // 2, 2)
    side_no = q // 2
    child = 1 - side_no
    n = s // 8
    slot = 4 * n + 2 * k + side_no
    partner = s + 1 - 2 * k
    near_slots = [4 * n + 2 * k + child, 4 - 4 * n + 2 * k + side_no, 4 - 4 * n + 2 * k + child]
    edge = s + 4 * side_no - 2
    mate = s + 2 - 4 * side_no
    mate_edge = s + 4 - 8 * side_no
    opposite = lax.rem(s + 8, 16)
    cross = 14 - s + 2 * k
    base = 8 * n
    ids = {
        "own": (s, s - base), "edge": (edge, edge - base),
        "mate": (mate, mate - base), "mate_edge": (mate_edge, mate_edge - base),
        "x_own": (cross, 0), "x_edge": (cross + 2 - 4 * side_no, 0),
        "x_mate": (cross - 2 + 4 * side_no, 0), "x_mate_edge": (cross - 4 + 8 * side_no, 0),
    }
    column = [lax.rem(s + i, 16) for i in range(16)]
    plane = [lax.rem(r + i, 16) for i in range(16)]
    eighth = [lax.rem(r + i, 8) for i in range(8)]
    root_home = r // 8 == n

    barrier = pltpu.get_barrier_semaphore()
    for i in range(1, 16):
        pl.semaphore_signal(barrier, inc=1, device_id=(column[i], r), device_id_type=MESH)
    for i in range(1, 16):
        pl.semaphore_signal(barrier, inc=1, device_id=(s, plane[i]), device_id_type=MESH)

    def load(i):
        rows = pl.ds(i * 512, 512)
        return [
            pltpu.make_async_copy(d_hbm.at[rows], dv.at[i], load_sem.at[0, i]),
            pltpu.make_async_copy(b_hbm.at[rows], bv.at[i], load_sem.at[1, i]),
            pltpu.make_async_copy(u_hbm.at[rows], uv.at[i], load_sem.at[2, i]),
        ]

    def load_local(i):
        rows = pl.ds(i * 512, 512)
        return [
            pltpu.make_async_copy(lm_hbm.at[rows], lm.at[i], load_sem.at[3, i]),
            pltpu.make_async_copy(lw_hbm.at[rows], lw.at[i], load_sem.at[4, i]),
        ]

    for i in range(4):
        for c in load(i):
            c.start()
    for i in range(3):
        for c in load_local(i):
            c.start()
    place1 = pl.ds(k * 256, 256)
    other1 = pl.ds(256 - k * 256, 256)
    own2 = 2 * child + k
    beside2 = 2 * child + 1 - k
    edge2 = 2 - 2 * child + k
    beside_edge2 = 3 - 2 * child - k
    from_edge2 = 2 * side_no + k

    def part2(i):
        return pl.ds(i * 128, 128)

    here2 = part2(own2)
    edge_rows2 = part2(edge2)
    to_proc2 = part2(from_edge2)
    mate_set = pl.ds(64 - 64 * side_no, 64)
    first, second, third, fourth = pl.ds(0, 256), pl.ds(256, 128), pl.ds(384, 64), pl.ds(448, 32)
    own = [
        pltpu.make_async_copy(um_hbm.at[first], m1.at[place1], own_sem.at[0]),
        pltpu.make_async_copy(uw_hbm.at[first], w1.at[place1], own_sem.at[1]),
        pltpu.make_async_copy(um_hbm.at[second], m2.at[here2], own_sem.at[2]),
        pltpu.make_async_copy(uw_hbm.at[second], w2.at[here2], own_sem.at[3]),
        pltpu.make_async_copy(um_hbm.at[third], rm.at[s - base], own_sem.at[4]),
        pltpu.make_async_copy(uw_hbm.at[third], rw.at[s - base], own_sem.at[5]),
        pltpu.make_async_copy(um_hbm.at[fourth], xm.at[s], own_sem.at[6]),
        pltpu.make_async_copy(uw_hbm.at[fourth], xw.at[s], own_sem.at[7]),
        pltpu.make_async_copy(top_hbm, tp.at[s - base], own_sem.at[8]),
    ]
    for c in own:
        c.start()

    sent = {0: [], 1: [], 2: [], 3: []}
    sems = {0: proc_sem, 1: edge_sem, 2: both_sem, 3: root_send_sem}

    def copy_of(which, i):
        src, dst, sem, to = sent[which][i]
        src, dst, sem = at(src), at(dst), at(sem)
        return pltpu.make_async_remote_copy(
            src_ref=src, dst_ref=dst, send_sem=sems[which].at[i], recv_sem=sem,
            device_id=to, device_id_type=MESH,
        )

    def send(which, src, dst, sem, to):
        sent[which].append((src, dst, sem, to))
        copy_of(which, len(sent[which]) - 1).start()
        return len(sent[which]) - 1

    flushed = set()

    def flush(which, copies):
        for i in copies:
            copy_of(which, i).wait_send()
            flushed.add((which, i))

    def drain(which):
        for i in range(len(sent[which])):
            if (which, i) not in flushed:
                copy_of(which, i).wait_send()

    def arrived(dst, sem):
        pltpu.make_async_remote_copy(
            src_ref=dst, dst_ref=dst, send_sem=both_sem.at[0], recv_sem=sem,
            device_id=(partner, r), device_id_type=MESH,
        ).wait_recv()

    pl.semaphore_wait(barrier, 30)

    rings = (
        (V(um_hbm)[third], rm, 1), (V(uw_hbm)[third], rw, 1),
        (V(um_hbm)[fourth], xm, 0), (V(uw_hbm)[fourth], xw, 0), (top_hbm, tp, 1),
    )

    def spot(a, name):
        i = ids[name][rings[a][2]]
        return V(rings[a][1])[i], V(ring_sem)[a, i]

    def ring_own(which, arrays, to):
        for a in arrays:
            dst, sem = spot(a, "own")
            send(which, rings[a][0], dst, sem, (to, r))

    def relay(name, arrays, *to):
        for a in arrays:
            dst, sem = spot(a, name)
            arrived(at(dst), at(sem))
            for t in to:
                send(0, dst, dst, sem, (t, r))

    @pl.when(is_proc == 0)
    def _():
        send(1, V(um_hbm)[second], V(m2)[to_proc2], V(up_sem)[0, 2], (mate, r))
        send(1, V(uw_hbm)[second], V(w2)[to_proc2], V(up_sem)[1, 2], (mate, r))
        ring_own(1, (0, 1), mate)

    @pl.when(is_proc == 1)
    def _():
        ring_own(0, (0, 1, 2, 3), mate)
        ring_own(0, (2, 3), cross)

    send(2, V(um_hbm)[first], V(m1)[place1], V(up_sem)[2, 0], (partner, r))
    send(2, V(uw_hbm)[first], V(w1)[place1], V(up_sem)[3, 0], (partner, r))

    @pl.when(is_proc == 1)
    def _():
        send(0, V(um_hbm)[second], V(m2)[here2], V(up_sem)[0, 1], (partner, r))
        send(0, V(uw_hbm)[second], V(w2)[here2], V(up_sem)[1, 1], (partner, r))
        ring_own(0, (0, 1, 2, 3, 4), partner)
        ring_own(0, (4,), mate)

    def leaf_up(i, carry):
        for c in load(i):
            c.wait()
        solved = mul(dv[i], bv[i]).astype(BF)
        cl[i] = t_mul(solved, uv[i]).astype(BF)
        return carry

    lax.fori_loop(0, 4, leaf_up, 0)

    def node_up(pair, m, w):
        inner = mul_t(pair, m).astype(BF)
        return mul(inner, w).astype(BF)

    def node_down(pair, t, m, w):
        x = (pair.astype(F32) - mul_t(t, w)).astype(BF)
        return mul_t(x, m).astype(BF)

    def side(ref, i):
        return jnp.concatenate([ref[2 * i], ref[2 * i + 1]], axis=1)

    def local_up(i, carry):
        for c in load_local(i):
            c.wait()
        cn[i] = node_up(side(cl, i), lm[i], lw[i])
        return carry

    lax.fori_loop(0, 2, local_up, 0)
    for c in load_local(2):
        c.wait()
    ct[...] = node_up(side(cn, 0), lm[2], lw[2])

    send(2, V(ct)[pl.ds(128 - 128 * k, 128)], V(p1)[k], V(small_sem)[0], (partner, r))
    p1[k] = ct[pl.ds(pl.multiple_of(128 * k, 128), 128), :]
    for c in own:
        c.wait()
    arrived(m1.at[other1], up_sem.at[2, 0])
    arrived(w1.at[other1], up_sem.at[3, 0])
    arrived(p1.at[1 - k], small_sem.at[0])
    c1[...] = node_up(side(p1, 0), m1[...], w1[...])

    def own_gain(e):
        m1h = m1[pl.ds(pl.multiple_of(256 * k, 256), 256), :]
        e = mul(m1h, mul(w1[...], e).astype(BF)).astype(BF)
        lo = mul(lm[2], mul(lw[2], e).astype(BF)).astype(BF)
        for n in range(2):
            half = lo[256 * n : 256 * n + 256]
            e2 = mul(lm[n], mul(lw[n], half).astype(BF)).astype(BF)
            for j in range(2):
                i = 2 * n + j
                ue = mul(uv[i], e2[256 * j : 256 * j + 256, :]).astype(BF)
                hv[i] = mul(dv[i], ue).astype(BF)

    @pl.when(is_proc == 0)
    def _():
        send(1, c1, V(p2)[side_no], V(small_sem)[1], (mate, r))
        ring_own(1, (2, 3, 4), mate)
        arrived(kr, small_sem.at[10])
        own_gain(kr[...])
        arrived(f1, small_sem.at[11])

    @pl.when(is_proc == 1)
    def _():
        p2[child] = c1[...]
        arrived(m2.at[part2(edge2)], up_sem.at[0, 2])
        send(0, V(m2)[edge_rows2], V(m2)[edge_rows2], V(up_sem)[0, 3], (partner, r))
        arrived(w2.at[part2(edge2)], up_sem.at[1, 2])
        send(0, V(w2)[edge_rows2], V(w2)[edge_rows2], V(up_sem)[1, 3], (partner, r))
        relay("mate", (0, 1), partner)
        relay("mate", (2, 3), partner, cross)
        relay("edge", (0, 1), mate, partner)
        for i, c in ((1, beside2), (3, beside_edge2)):
            arrived(m2.at[part2(c)], up_sem.at[0, i])
            arrived(w2.at[part2(c)], up_sem.at[1, i])
        arrived(p2.at[1 - child], small_sem.at[1])
        c2[...] = node_up(side(p2, 0), m2[...], w2[...])
        send(0, V(c2)[mate_set], V(p3)[side_no], V(small_sem)[2], (mate, r))
        p3[side_no] = c2[pl.ds(pl.multiple_of(64 * side_no, 64), 64), :]
        relay("edge", (2, 3), mate, partner, cross)
        relay("mate_edge", (0, 1), partner)
        for a in (0, 1):
            for i in range(4):
                j = lax.rem(partner + 2 * i, 8)
                arrived(rings[a][1].at[j], ring_sem.at[a, j])
        arrived(p3.at[1 - side_no], small_sem.at[2])
        m3 = rm[...].reshape(512, 512)
        w3 = rw[...].reshape(512, 256)
        pair3 = side(p3, 0)
        p4[n] = node_up(pair3, m3, w3)
        send(0, V(p4)[n], V(p4)[n], V(small_sem)[3], (opposite, r))
        relay("mate_edge", (2, 3), partner, cross)
        relay("edge", (4,), mate, partner)
        relay("mate", (4,), partner)
        for name in ("x_own", "x_mate", "x_edge", "x_mate_edge"):
            relay(name, (2, 3), partner)
        for a in (2, 3):
            for i in range(8):
                j = lax.rem(partner + 2 * i, 16)
                arrived(rings[a][1].at[j], ring_sem.at[a, j])
        arrived(p4.at[1 - n], small_sem.at[3])
        w4 = xw[...].reshape(512, 256)
        inner4 = mul_t(side(p4, 0), xm[...].reshape(512, 512)).astype(BF)
        root = mul(inner4, w4).astype(BF)

        @pl.when(root_home)
        def _():
            rt[eighth[0]] = root
            for i in range(1, 16):
                send(3, V(rt)[eighth[0]], V(rt)[eighth[0]], V(root_sem)[eighth[0]], (s, plane[i]))

        t3 = jnp.where(n == 0, inner4[:, :256], inner4[:, 256:])
        t2 = node_down(pair3, t3, m3, w3)
        t2s[0] = t2[:, :256]
        t2s[1] = t2[:, 256:]
        send(0, V(t2s)[child], V(f2)[side_no], V(small_sem)[6], (mate, r))
        f2[side_no] = t2s[side_no]
        relay("mate_edge", (4,), partner)

        m4h = xm[pl.ds(base, 8)].reshape(256, 512)
        e = mul(m4h, w4).astype(BF)
        m3h = rm[pl.ds(4 * side_no, 4)].reshape(256, 512)
        e = mul(m3h, mul(w3, e).astype(BF)).astype(BF)
        lifted2 = mul(w2[...], e).astype(BF)
        m2_edge = m2[pl.ds(pl.multiple_of(256 - 256 * child, 256), 256), :]
        ks[...] = mul(m2_edge, lifted2).astype(BF)
        send(0, ks, kr, V(small_sem)[10], (edge, r))
        m2_own = m2[pl.ds(pl.multiple_of(256 * child, 256), 256), :]
        own_gain(mul(m2_own, lifted2).astype(BF))
        arrived(f2.at[child], small_sem.at[6])
        t1 = node_down(side(p2, 0), f2[...].reshape(128, 256), m2[...], w2[...])
        t1s[0] = t1[:, :256]
        t1s[1] = t1[:, 256:]
        send(0, V(t1s)[side_no], f1, V(small_sem)[11], (edge, r))
        f1[...] = t1s[child]
        for i in range(4):
            j = lax.rem(partner + 2 * i, 8)
            arrived(tp.at[j], ring_sem.at[4, j])

        for i in range(1, 8):
            arrived(rt.at[eighth[i]], root_sem.at[eighth[i]])

        @pl.when(jnp.logical_not(root_home))
        def _():
            arrived(rt.at[eighth[0]], root_sem.at[eighth[0]])

        total = mul_t(rt[0], tp[0])
        for j in range(1, 8):
            total += mul_t(rt[j], tp[j])
        t4[slot] = total.astype(BF)
        for i in range(1, 8):
            send(0, V(t4)[slot], V(t4)[slot], V(t4_sem)[slot], (column[2 * i], r))
        send(0, V(t4)[slot], V(t4)[slot], V(t4_sem)[slot], (partner, r))

    t0 = node_down(side(p1, 0), f1[...], m1[...], w1[...])
    t0s[0] = t0[:, :256]
    t0s[1] = t0[:, 256:]
    send(2, V(t0s)[1 - k], V(f0)[k], V(small_sem)[12], (partner, r))
    f0[k] = t0s[k]
    arrived(f0.at[1 - k], small_sem.at[12])
    ta = node_down(side(cn, 0), f0[...].reshape(256, 256), lm[2], lw[2])
    for n in range(2):
        tb = node_down(side(cl, n), ta[:, 256 * n : 256 * n + 256], lm[n], lw[n])
        for j in range(2):
            i = 2 * n + j
            x = (bv[i].astype(F32) - mul_t(uv[i], tb[:, 256 * j : 256 * j + 256])).astype(BF)
            sv[i] = mul(dv[i], x)

    def pass_on(which, i):
        arrived(t4.at[i], t4_sem.at[i])
        send(which, V(t4)[i], V(t4)[i], V(t4_sem)[i], (partner, r))

    @pl.when(is_proc == 0)
    def _():
        pass_on(1, slot)

    for i in near_slots:
        pass_on(2, i)
    for i in range(4):
        j = 4 * (i // 2) + 2 - 2 * k + i % 2
        arrived(t4.at[j], t4_sem.at[j])

    top = (t4[0:4].astype(F32) + t4[4:8].astype(F32)).astype(BF).reshape(256, 256)

    def last(i):
        return pltpu.make_async_copy(sv.at[i], out_hbm.at[pl.ds(i * 512, 512)], out_sem.at[i])

    def finish(i, carry):
        sv[i] = sv[i] - mul_t(hv[i], top)
        last(i).start()
        return carry

    lax.fori_loop(0, 4, finish, 0)
    drain(2)

    @pl.when(is_proc == 1)
    def _():
        drain(0)

        @pl.when(root_home)
        def _():
            drain(3)

    @pl.when(is_proc == 0)
    def _():
        drain(1)

    for i in range(4):
        last(i).wait()


def body(b, d, u, lm, lw, um, uw, top):
    flat = [a.reshape(a.shape[-2:]) for a in (b, d, u, lm, lw, um, uw, top)]
    dma = pltpu.SemaphoreType.DMA
    vm = pltpu.VMEM
    out = pl.pallas_call(
        kernel,
        out_shape=jax.ShapeDtypeStruct((2048, 256), F32),
        in_specs=[pl.BlockSpec(memory_space=pl.ANY)] * 8,
        out_specs=pl.BlockSpec(memory_space=pl.ANY),
        scratch_shapes=[
            vm((4, 512, 256), BF), vm((4, 512, 512), BF), vm((4, 512, 256), BF),
            vm((3, 512, 512), BF), vm((3, 512, 256), BF),
            vm((512, 512), BF), vm((512, 256), BF), vm((512, 512), BF), vm((512, 256), BF),
            vm((8, 64, 512), BF), vm((8, 64, 256), BF), vm((16, 32, 512), BF), vm((16, 32, 256), BF),
            vm((8, 256, 256), BF),
            vm((4, 256, 256), BF), vm((2, 256, 256), BF), vm((256, 256), BF),
            vm((2, 128, 256), BF), vm((2, 128, 256), BF), vm((128, 256), BF), vm((128, 256), BF),
            vm((2, 64, 256), BF), vm((2, 64, 256), BF), vm((8, 64, 256), BF), vm((8, 64, 256), BF),
            vm((2, 64, 256), BF), vm((2, 64, 256), BF), vm((2, 128, 256), BF), vm((128, 256), BF),
            vm((2, 128, 256), BF), vm((2, 128, 256), BF), vm((256, 256), BF), vm((256, 256), BF),
            vm((4, 512, 256), F32), vm((4, 512, 256), BF),
            dma((5, 4)), dma((9,)), dma((4,)), dma((7,)), dma((92,)), dma((9,)), dma((15,)),
            dma((4, 4)), dma((5, 16)), dma((13,)), dma((8,)), dma((8,)),
        ],
        compiler_params=pltpu.CompilerParams(
            collective_id=0, has_side_effects=True, vmem_limit_bytes=56 << 20
        ),
    )(*flat)
    return out.reshape(1, 2048, 256)


def solution(mesh):
    rows = P("root", "sub", None)
    return jax.shard_map(
        body, mesh=mesh, in_specs=(rows,) * 7 + (P("root", "sub"),), out_specs=rows, check_vma=False
    )
```

```python
import jax
import jax.numpy as jnp
from jax import lax
from jax.experimental import pallas as pl
from jax.experimental.pallas import tpu as pltpu
from jax.sharding import PartitionSpec as P

MESH = pl.DeviceIdType.MESH
BF = jnp.bfloat16
F32 = jnp.float32


def mul(a, b):
    return lax.dot_general(a, b, (((1,), (0,)), ((), ())), preferred_element_type=F32)


def mul_t(a, b):
    return lax.dot_general(a, b, (((1,), (1,)), ((), ())), preferred_element_type=F32)


def t_mul(a, b):
    return lax.dot_general(a, b, (((0,), (0,)), ((), ())), preferred_element_type=F32)


class V:
    def __init__(self, ref, index=None):
        self.ref, self.index = ref, index

    def __getitem__(self, index):
        return V(self.ref, index)


def at(view):
    return view.ref.at[view.index] if isinstance(view, V) else view


def kernel(
    b_hbm, d_hbm, u_hbm, lm_hbm, lw_hbm, um_hbm, uw_hbm, top_hbm,
    sv, hv, top,
    bv, dv, uv, lm, lw, m1, w1, m2, w2, rm, rw, xm, xw, tp,
    cl, cn, ct, p1, p2, c1, c2, p3, p4, rt, t4,
    t2s, f2, t1s, f1, t0s, f0, ks, kr,
    load_sem, own_sem, both_sem, proc_sem, edge_sem, root_send_sem,
    up_sem, ring_sem, small_sem, root_sem, t4_sem,
):
    s = lax.axis_index("sub")
    r = lax.axis_index("root")
    k = lax.rem(s, 2)
    q = lax.rem(s // 2, 4)
    is_proc = lax.rem((q + 1) // 2, 2)
    side_no = q // 2
    child = 1 - side_no
    n = s // 8
    slot = 4 * n + 2 * k + side_no
    partner = s + 1 - 2 * k
    near_slots = [4 * n + 2 * k + child, 4 - 4 * n + 2 * k + side_no, 4 - 4 * n + 2 * k + child]
    edge = s + 4 * side_no - 2
    mate = s + 2 - 4 * side_no
    mate_edge = s + 4 - 8 * side_no
    opposite = lax.rem(s + 8, 16)
    cross = 14 - s + 2 * k
    base = 8 * n
    far = lax.rem(s + 12 + 8 * side_no, 16)
    ids = {
        "own": (s, s - base), "edge": (edge, edge - base),
        "mate": (mate, mate - base), "mate_edge": (mate_edge, mate_edge - base),
        "x_own": (cross, 0), "x_edge": (cross + 2 - 4 * side_no, 0),
        "x_mate": (cross - 2 + 4 * side_no, 0), "x_mate_edge": (cross - 4 + 8 * side_no, 0),
    }
    column = [lax.rem(s + i, 16) for i in range(16)]
    far_first = sorted(
        [(dy, dx) for dy in range(4) for dx in range(4) if dy or dx],
        key=lambda d: -min(d[0], 4 - d[0]) - min(d[1], 4 - d[1]),
    )
    plane = [4 * lax.rem(r // 4 + dy, 4) + lax.rem(r + dx, 4) for dy, dx in far_first]
    eighth = [lax.rem(r + i, 8) for i in range(8)]
    root_home = r // 8 == n

    barrier = pltpu.get_barrier_semaphore()
    for i in range(1, 16):
        pl.semaphore_signal(barrier, inc=1, device_id=(column[i], r), device_id_type=MESH)
    for i in range(15):
        pl.semaphore_signal(barrier, inc=1, device_id=(s, plane[i]), device_id_type=MESH)

    def load(i):
        rows = pl.ds(i * 512, 512)
        return [
            pltpu.make_async_copy(d_hbm.at[rows], dv.at[i], load_sem.at[0, i]),
            pltpu.make_async_copy(b_hbm.at[rows], bv.at[i], load_sem.at[1, i]),
            pltpu.make_async_copy(u_hbm.at[rows], uv.at[i], load_sem.at[2, i]),
        ]

    def load_local(i):
        rows = pl.ds(i * 512, 512)
        return [
            pltpu.make_async_copy(lm_hbm.at[rows], lm.at[i], load_sem.at[3, i]),
            pltpu.make_async_copy(lw_hbm.at[rows], lw.at[i], load_sem.at[4, i]),
        ]

    for i in range(4):
        for c in load(i):
            c.start()
    for i in range(3):
        for c in load_local(i):
            c.start()
    place1 = pl.ds(k * 256, 256)
    other1 = pl.ds(256 - k * 256, 256)
    own2 = 2 * child + k
    beside2 = 2 * child + 1 - k
    edge2 = 2 - 2 * child + k
    beside_edge2 = 3 - 2 * child - k
    from_edge2 = 2 * side_no + k

    def part2(i):
        return pl.ds(i * 128, 128)

    here2 = part2(own2)
    edge_rows2 = part2(edge2)
    to_proc2 = part2(from_edge2)
    mate_set = pl.ds(64 - 64 * side_no, 64)
    first, second, third, fourth = pl.ds(0, 256), pl.ds(256, 128), pl.ds(384, 64), pl.ds(448, 32)
    own = [
        pltpu.make_async_copy(um_hbm.at[first], m1.at[place1], own_sem.at[0]),
        pltpu.make_async_copy(uw_hbm.at[first], w1.at[place1], own_sem.at[1]),
        pltpu.make_async_copy(um_hbm.at[second], m2.at[here2], own_sem.at[2]),
        pltpu.make_async_copy(uw_hbm.at[second], w2.at[here2], own_sem.at[3]),
        pltpu.make_async_copy(um_hbm.at[third], rm.at[s - base], own_sem.at[4]),
        pltpu.make_async_copy(uw_hbm.at[third], rw.at[s - base], own_sem.at[5]),
        pltpu.make_async_copy(um_hbm.at[fourth], xm.at[s], own_sem.at[6]),
        pltpu.make_async_copy(uw_hbm.at[fourth], xw.at[s], own_sem.at[7]),
        pltpu.make_async_copy(top_hbm, tp.at[s - base], own_sem.at[8]),
    ]
    for c in own:
        c.start()

    sent = {0: [], 1: [], 2: [], 3: []}
    sems = {0: proc_sem, 1: edge_sem, 2: both_sem, 3: root_send_sem}

    def copy_of(which, i):
        src, dst, sem, to = sent[which][i]
        src, dst, sem = at(src), at(dst), at(sem)
        return pltpu.make_async_remote_copy(
            src_ref=src, dst_ref=dst, send_sem=sems[which].at[i], recv_sem=sem,
            device_id=to, device_id_type=MESH,
        )

    def send(which, src, dst, sem, to):
        sent[which].append((src, dst, sem, to))
        copy_of(which, len(sent[which]) - 1).start()
        return len(sent[which]) - 1

    flushed = set()

    def flush(which, copies):
        for i in copies:
            copy_of(which, i).wait_send()
            flushed.add((which, i))

    def drain(which):
        for i in range(len(sent[which])):
            if (which, i) not in flushed:
                copy_of(which, i).wait_send()

    def arrived(dst, sem):
        pltpu.make_async_remote_copy(
            src_ref=dst, dst_ref=dst, send_sem=both_sem.at[0], recv_sem=sem,
            device_id=(partner, r), device_id_type=MESH,
        ).wait_recv()

    pl.semaphore_wait(barrier, 30)

    rings = (
        (V(um_hbm)[third], rm, 1), (V(uw_hbm)[third], rw, 1),
        (V(um_hbm)[fourth], xm, 0), (V(uw_hbm)[fourth], xw, 0), (top_hbm, tp, 1),
    )

    def spot(a, name):
        i = ids[name][rings[a][2]]
        return V(rings[a][1])[i], V(ring_sem)[a, i]

    def ring_own(which, arrays, to):
        for a in arrays:
            dst, sem = spot(a, "own")
            send(which, rings[a][0], dst, sem, (to, r))

    def relay(name, arrays, *to):
        for a in arrays:
            dst, sem = spot(a, name)
            arrived(at(dst), at(sem))
            for t in to:
                send(0, dst, dst, sem, (t, r))

    @pl.when(is_proc == 0)
    def _():
        ring_own(1, (0, 1), mate)
        send(1, V(um_hbm)[second], V(m2)[to_proc2], V(up_sem)[0, 2], (mate, r))
        send(1, V(uw_hbm)[second], V(w2)[to_proc2], V(up_sem)[1, 2], (mate, r))
        ring_own(1, (2, 3), far)

    @pl.when(is_proc == 1)
    def _():
        ring_own(0, (0, 1, 2, 3), mate)
        ring_own(0, (2, 3), cross)

    send(2, V(um_hbm)[first], V(m1)[place1], V(up_sem)[2, 0], (partner, r))
    send(2, V(uw_hbm)[first], V(w1)[place1], V(up_sem)[3, 0], (partner, r))

    @pl.when(is_proc == 1)
    def _():
        send(0, V(um_hbm)[second], V(m2)[here2], V(up_sem)[0, 1], (partner, r))
        send(0, V(uw_hbm)[second], V(w2)[here2], V(up_sem)[1, 1], (partner, r))
        ring_own(0, (0, 1, 2, 3, 4), partner)
        ring_own(0, (4,), mate)

    def leaf_up(i, carry):
        for c in load(i):
            c.wait()
        solved = mul(dv[i], bv[i]).astype(BF)
        cl[i] = t_mul(solved, uv[i]).astype(BF)
        return carry

    lax.fori_loop(0, 4, leaf_up, 0)

    def node_up(pair, m, w):
        inner = mul_t(pair, m).astype(BF)
        return mul(inner, w).astype(BF)

    def node_down(pair, t, m, w):
        x = (pair.astype(F32) - mul_t(t, w)).astype(BF)
        return mul_t(x, m).astype(BF)

    def side(ref, i):
        return jnp.concatenate([ref[2 * i], ref[2 * i + 1]], axis=1)

    def local_up(i, carry):
        for c in load_local(i):
            c.wait()
        cn[i] = node_up(side(cl, i), lm[i], lw[i])
        return carry

    lax.fori_loop(0, 2, local_up, 0)
    for c in load_local(2):
        c.wait()
    ct[...] = node_up(side(cn, 0), lm[2], lw[2])

    send(2, V(ct)[pl.ds(128 - 128 * k, 128)], V(p1)[k], V(small_sem)[0], (partner, r))
    p1[k] = ct[pl.ds(pl.multiple_of(128 * k, 128), 128), :]
    for c in own:
        c.wait()
    arrived(m1.at[other1], up_sem.at[2, 0])
    arrived(w1.at[other1], up_sem.at[3, 0])
    arrived(p1.at[1 - k], small_sem.at[0])
    c1[...] = node_up(side(p1, 0), m1[...], w1[...])

    def own_gain(e):
        m1h = m1[pl.ds(pl.multiple_of(256 * k, 256), 256), :]
        e = mul(m1h, mul(w1[...], e).astype(BF)).astype(BF)
        lo = mul(lm[2], mul(lw[2], e).astype(BF)).astype(BF)
        for n in range(2):
            half = lo[256 * n : 256 * n + 256]
            e2 = mul(lm[n], mul(lw[n], half).astype(BF)).astype(BF)
            for j in range(2):
                i = 2 * n + j
                ue = mul(uv[i], e2[256 * j : 256 * j + 256, :]).astype(BF)
                hv[i] = mul(dv[i], ue).astype(BF)

    @pl.when(is_proc == 0)
    def _():
        first_sent = send(1, c1, V(p2)[side_no], V(small_sem)[1], (mate, r))
        flush(1, [first_sent])
        ring_own(1, (2, 3, 4), mate)
        arrived(kr, small_sem.at[10])
        own_gain(kr[...])
        arrived(f1, small_sem.at[11])

    @pl.when(is_proc == 1)
    def _():
        p2[child] = c1[...]
        relay("edge", (0, 1), mate, partner)
        arrived(m2.at[part2(edge2)], up_sem.at[0, 2])
        send(0, V(m2)[edge_rows2], V(m2)[edge_rows2], V(up_sem)[0, 3], (partner, r))
        arrived(w2.at[part2(edge2)], up_sem.at[1, 2])
        send(0, V(w2)[edge_rows2], V(w2)[edge_rows2], V(up_sem)[1, 3], (partner, r))
        relay("mate", (0, 1), partner)
        relay("mate", (2, 3), partner)
        relay("x_own", (2, 3), mate, partner)
        relay("x_edge", (2, 3), mate, partner)
        for i, c in ((1, beside2), (3, beside_edge2)):
            arrived(m2.at[part2(c)], up_sem.at[0, i])
            arrived(w2.at[part2(c)], up_sem.at[1, i])
        arrived(p2.at[1 - child], small_sem.at[1])
        c2[...] = node_up(side(p2, 0), m2[...], w2[...])
        send(0, V(c2)[mate_set], V(p3)[side_no], V(small_sem)[2], (mate, r))
        p3[side_no] = c2[pl.ds(pl.multiple_of(64 * side_no, 64), 64), :]
        relay("mate_edge", (0, 1), partner)
        for a in (0, 1):
            for i in range(4):
                j = lax.rem(partner + 2 * i, 8)
                arrived(rings[a][1].at[j], ring_sem.at[a, j])
        arrived(p3.at[1 - side_no], small_sem.at[2])
        m3 = rm[...].reshape(512, 512)
        w3 = rw[...].reshape(512, 256)
        pair3 = side(p3, 0)
        p4[n] = node_up(pair3, m3, w3)
        send(0, V(p4)[n], V(p4)[n], V(small_sem)[3], (opposite, r))
        relay("x_mate", (2, 3), partner)
        relay("x_mate_edge", (2, 3), partner)
        relay("edge", (2, 3), mate, partner)
        relay("edge", (4,), mate, partner)
        relay("mate_edge", (2, 3), partner)
        for a in (2, 3):
            for i in range(8):
                j = lax.rem(partner + 2 * i, 16)
                arrived(rings[a][1].at[j], ring_sem.at[a, j])
        arrived(p4.at[1 - n], small_sem.at[3])
        w4 = xw[...].reshape(512, 256)
        inner4 = mul_t(side(p4, 0), xm[...].reshape(512, 512)).astype(BF)
        root = mul(inner4, w4).astype(BF)

        @pl.when(root_home)
        def _():
            rt[eighth[0]] = root
            for i in range(15):
                send(3, V(rt)[eighth[0]], V(rt)[eighth[0]], V(root_sem)[eighth[0]], (s, plane[i]))

        t3 = jnp.where(n == 0, inner4[:, :256], inner4[:, 256:])
        t2 = node_down(pair3, t3, m3, w3)
        t2s[0] = t2[:, :256]
        t2s[1] = t2[:, 256:]
        send(0, V(t2s)[child], V(f2)[side_no], V(small_sem)[6], (mate, r))
        f2[side_no] = t2s[side_no]
        relay("mate", (4,), partner)
        relay("mate_edge", (4,), partner)

        m4h = xm[pl.ds(base, 8)].reshape(256, 512)
        e = mul(m4h, w4).astype(BF)
        m3h = rm[pl.ds(4 * side_no, 4)].reshape(256, 512)
        e = mul(m3h, mul(w3, e).astype(BF)).astype(BF)
        lifted2 = mul(w2[...], e).astype(BF)
        m2_edge = m2[pl.ds(pl.multiple_of(256 - 256 * child, 256), 256), :]
        ks[...] = mul(m2_edge, lifted2).astype(BF)
        send(0, ks, kr, V(small_sem)[10], (edge, r))
        m2_own = m2[pl.ds(pl.multiple_of(256 * child, 256), 256), :]
        own_gain(mul(m2_own, lifted2).astype(BF))
        arrived(f2.at[child], small_sem.at[6])
        t1 = node_down(side(p2, 0), f2[...].reshape(128, 256), m2[...], w2[...])
        t1s[0] = t1[:, :256]
        t1s[1] = t1[:, 256:]
        send(0, V(t1s)[side_no], f1, V(small_sem)[11], (edge, r))
        f1[...] = t1s[child]
        for i in range(4):
            j = lax.rem(partner + 2 * i, 8)
            arrived(tp.at[j], ring_sem.at[4, j])

        for i in range(1, 8):
            arrived(rt.at[eighth[i]], root_sem.at[eighth[i]])

        @pl.when(jnp.logical_not(root_home))
        def _():
            arrived(rt.at[eighth[0]], root_sem.at[eighth[0]])

        total = mul_t(rt[0], tp[0])
        for j in range(1, 8):
            total += mul_t(rt[j], tp[j])
        t4[slot] = total.astype(BF)
        for i in (4, 3, 5, 2, 6, 1, 7):
            send(0, V(t4)[slot], V(t4)[slot], V(t4_sem)[slot], (column[2 * i], r))
        send(0, V(t4)[slot], V(t4)[slot], V(t4_sem)[slot], (partner, r))

    t0 = node_down(side(p1, 0), f1[...], m1[...], w1[...])
    t0s[0] = t0[:, :256]
    t0s[1] = t0[:, 256:]
    send(2, V(t0s)[1 - k], V(f0)[k], V(small_sem)[12], (partner, r))
    f0[k] = t0s[k]
    arrived(f0.at[1 - k], small_sem.at[12])
    ta = node_down(side(cn, 0), f0[...].reshape(256, 256), lm[2], lw[2])
    for n in range(2):
        tb = node_down(side(cl, n), ta[:, 256 * n : 256 * n + 256], lm[n], lw[n])
        for j in range(2):
            i = 2 * n + j
            x = (bv[i].astype(F32) - mul_t(uv[i], tb[:, 256 * j : 256 * j + 256])).astype(BF)
            sv[i] = mul(dv[i], x)

    def pass_on(which, i):
        arrived(t4.at[i], t4_sem.at[i])
        send(which, V(t4)[i], V(t4)[i], V(t4_sem)[i], (partner, r))

    @pl.when(is_proc == 0)
    def _():
        pass_on(1, slot)

    for i in near_slots:
        pass_on(2, i)
    for i in range(4):
        j = 4 * (i // 2) + 2 - 2 * k + i % 2
        arrived(t4.at[j], t4_sem.at[j])

    top[...] = (t4[0:4].astype(F32) + t4[4:8].astype(F32)).astype(BF).reshape(256, 256)
    drain(2)

    @pl.when(is_proc == 1)
    def _():
        drain(0)

        @pl.when(root_home)
        def _():
            drain(3)

    @pl.when(is_proc == 0)
    def _():
        drain(1)


def final_kernel(sv, hv, top, out_hbm, ov, out_sem):
    def last(i):
        return pltpu.make_async_copy(ov.at[i], out_hbm.at[pl.ds(i * 256, 256)], out_sem.at[i])

    def finish(i, carry):
        rows = pl.ds(pl.multiple_of(256 * lax.rem(i, 2), 256), 256)
        ov[i] = sv[i // 2, rows, :] - mul_t(hv[i // 2, rows, :], top[...])
        last(i).start()
        return carry

    lax.fori_loop(0, 8, finish, 0)
    for i in range(8):
        last(i).wait()


def body(b, d, u, lm, lw, um, uw, top):
    flat = [
        pltpu.with_memory_space_constraint(a.reshape(a.shape[-2:]), pltpu.HBM)
        for a in (b, d, u, lm, lw, um, uw, top)
    ]
    dma = pltpu.SemaphoreType.DMA
    vm = pltpu.VMEM
    inside = pl.BlockSpec(memory_space=pltpu.VMEM)
    parts = pl.pallas_call(
        kernel,
        out_shape=(
            jax.ShapeDtypeStruct((4, 512, 256), F32), jax.ShapeDtypeStruct((4, 512, 256), BF),
            jax.ShapeDtypeStruct((256, 256), BF),
        ),
        in_specs=[pl.BlockSpec(memory_space=pltpu.HBM)] * 8,
        out_specs=(inside,) * 3,
        scratch_shapes=[
            vm((4, 512, 256), BF), vm((4, 512, 512), BF), vm((4, 512, 256), BF),
            vm((3, 512, 512), BF), vm((3, 512, 256), BF),
            vm((512, 512), BF), vm((512, 256), BF), vm((512, 512), BF), vm((512, 256), BF),
            vm((8, 64, 512), BF), vm((8, 64, 256), BF), vm((16, 32, 512), BF), vm((16, 32, 256), BF),
            vm((8, 256, 256), BF),
            vm((4, 256, 256), BF), vm((2, 256, 256), BF), vm((256, 256), BF),
            vm((2, 128, 256), BF), vm((2, 128, 256), BF), vm((128, 256), BF), vm((128, 256), BF),
            vm((2, 64, 256), BF), vm((2, 64, 256), BF), vm((8, 64, 256), BF), vm((8, 64, 256), BF),
            vm((2, 64, 256), BF), vm((2, 64, 256), BF), vm((2, 128, 256), BF), vm((128, 256), BF),
            vm((2, 128, 256), BF), vm((2, 128, 256), BF), vm((256, 256), BF), vm((256, 256), BF),
            dma((5, 4)), dma((9,)), dma((7,)), dma((61,)), dma((11,)), dma((15,)),
            dma((4, 4)), dma((5, 16)), dma((13,)), dma((8,)), dma((8,)),
        ],
        compiler_params=pltpu.CompilerParams(
            collective_id=0, has_side_effects=True, vmem_limit_bytes=24 << 20
        ),
    )(*flat)
    out = pl.pallas_call(
        final_kernel,
        out_shape=jax.ShapeDtypeStruct((2048, 256), F32),
        in_specs=[inside] * 3,
        out_specs=pl.BlockSpec(memory_space=pl.ANY),
        scratch_shapes=[vm((8, 256, 256), F32), dma((8,))],
        compiler_params=pltpu.CompilerParams(vmem_limit_bytes=16 << 20),
    )(*parts)
    return out.reshape(1, 2048, 256)


def solution(mesh):
    rows = P("root", "sub", None)
    return jax.shard_map(
        body, mesh=mesh, in_specs=(rows,) * 7 + (P("root", "sub"),), out_specs=rows, check_vma=False
    )
```

```python
import jax
import jax.numpy as jnp
from jax import lax
from jax.experimental import pallas as pl
from jax.experimental.pallas import tpu as pltpu
from jax.sharding import PartitionSpec as P

MESH = pl.DeviceIdType.MESH
BF = jnp.bfloat16
F32 = jnp.float32


def mul(a, b):
    return lax.dot_general(a, b, (((1,), (0,)), ((), ())), preferred_element_type=F32)


def mul_t(a, b):
    return lax.dot_general(a, b, (((1,), (1,)), ((), ())), preferred_element_type=F32)


def t_mul(a, b):
    return lax.dot_general(a, b, (((0,), (0,)), ((), ())), preferred_element_type=F32)


class V:
    def __init__(self, ref, index=None):
        self.ref, self.index = ref, index

    def __getitem__(self, index):
        return V(self.ref, index)


def at(view):
    return view.ref.at[view.index] if isinstance(view, V) else view


def kernel(
    b_hbm, d_hbm, u_hbm, lm_hbm, lw_hbm, um_hbm, uw_hbm, top_hbm,
    sv, hv, top,
    bv, dv, uv, lm, lw, m1, w1, m2, w2, rm, rw, xm, xw, tp,
    cl, cn, ct, p1, p2, c1, c2, p3, p4, rt, t4,
    t2s, f2, t1s, f1, t0s, f0, ks, kr,
    load_sem, own_sem, both_sem, proc_sem, edge_sem, root_send_sem,
    up_sem, ring_sem, small_sem, root_sem, t4_sem,
):
    s = lax.axis_index("sub")
    r = lax.axis_index("root")
    k = lax.rem(s, 2)
    q = lax.rem(s // 2, 4)
    is_proc = lax.rem((q + 1) // 2, 2)
    side_no = q // 2
    child = 1 - side_no
    n = s // 8
    slot = 4 * n + 2 * k + side_no
    partner = s + 1 - 2 * k
    near_slots = [4 * n + 2 * k + child, 4 - 4 * n + 2 * k + side_no, 4 - 4 * n + 2 * k + child]
    edge = s + 4 * side_no - 2
    mate = s + 2 - 4 * side_no
    mate_edge = s + 4 - 8 * side_no
    opposite = lax.rem(s + 8, 16)
    cross = 14 - s + 2 * k
    base = 8 * n
    far = lax.rem(s + 12 + 8 * side_no, 16)
    ids = {
        "own": (s, s - base), "edge": (edge, edge - base),
        "mate": (mate, mate - base), "mate_edge": (mate_edge, mate_edge - base),
        "x_own": (cross, 0), "x_edge": (cross + 2 - 4 * side_no, 0),
        "x_mate": (cross - 2 + 4 * side_no, 0), "x_mate_edge": (cross - 4 + 8 * side_no, 0),
    }
    column = [lax.rem(s + i, 16) for i in range(16)]
    far_first = sorted(
        [(dy, dx) for dy in range(4) for dx in range(4) if dy or dx],
        key=lambda d: -min(d[0], 4 - d[0]) - min(d[1], 4 - d[1]),
    )
    plane = [4 * lax.rem(r // 4 + dy, 4) + lax.rem(r + dx, 4) for dy, dx in far_first]
    eighth = [lax.rem(r + i, 8) for i in range(8)]
    root_home = r // 8 == n

    barrier = pltpu.get_barrier_semaphore()
    for i in range(1, 16):
        pl.semaphore_signal(barrier, inc=1, device_id=(column[i], r), device_id_type=MESH)
    for i in range(15):
        pl.semaphore_signal(barrier, inc=1, device_id=(s, plane[i]), device_id_type=MESH)

    def load(i):
        rows = pl.ds(i * 512, 512)
        return [
            pltpu.make_async_copy(d_hbm.at[rows], dv.at[i], load_sem.at[0, i]),
            pltpu.make_async_copy(b_hbm.at[rows], bv.at[i], load_sem.at[1, i]),
            pltpu.make_async_copy(u_hbm.at[rows], uv.at[i], load_sem.at[2, i]),
        ]

    def load_local(i):
        rows = pl.ds(i * 512, 512)
        return [
            pltpu.make_async_copy(lm_hbm.at[rows], lm.at[i], load_sem.at[3, i]),
            pltpu.make_async_copy(lw_hbm.at[rows], lw.at[i], load_sem.at[4, i]),
        ]

    for i in range(4):
        for c in load(i):
            c.start()
    for i in range(3):
        for c in load_local(i):
            c.start()
    place1 = pl.ds(k * 256, 256)
    other1 = pl.ds(256 - k * 256, 256)
    own2 = 2 * child + k
    beside2 = 2 * child + 1 - k
    edge2 = 2 - 2 * child + k
    beside_edge2 = 3 - 2 * child - k
    from_edge2 = 2 * side_no + k

    def part2(i):
        return pl.ds(i * 128, 128)

    here2 = part2(own2)
    edge_rows2 = part2(edge2)
    to_proc2 = part2(from_edge2)
    mate_set = pl.ds(64 - 64 * side_no, 64)
    first, second, third, fourth = pl.ds(0, 256), pl.ds(256, 128), pl.ds(384, 64), pl.ds(448, 32)
    own = [
        pltpu.make_async_copy(um_hbm.at[first], m1.at[place1], own_sem.at[0]),
        pltpu.make_async_copy(uw_hbm.at[first], w1.at[place1], own_sem.at[1]),
        pltpu.make_async_copy(um_hbm.at[second], m2.at[here2], own_sem.at[2]),
        pltpu.make_async_copy(uw_hbm.at[second], w2.at[here2], own_sem.at[3]),
        pltpu.make_async_copy(um_hbm.at[third], rm.at[s - base], own_sem.at[4]),
        pltpu.make_async_copy(uw_hbm.at[third], rw.at[s - base], own_sem.at[5]),
        pltpu.make_async_copy(um_hbm.at[fourth], xm.at[s], own_sem.at[6]),
        pltpu.make_async_copy(uw_hbm.at[fourth], xw.at[s], own_sem.at[7]),
        pltpu.make_async_copy(top_hbm, tp.at[s - base], own_sem.at[8]),
    ]
    for c in own:
        c.start()

    sent = {0: [], 1: [], 2: [], 3: []}
    sems = {0: proc_sem, 1: edge_sem, 2: both_sem, 3: root_send_sem}

    def copy_of(which, i):
        src, dst, sem, to = sent[which][i]
        src, dst, sem = at(src), at(dst), at(sem)
        return pltpu.make_async_remote_copy(
            src_ref=src, dst_ref=dst, send_sem=sems[which].at[i], recv_sem=sem,
            device_id=to, device_id_type=MESH,
        )

    def send(which, src, dst, sem, to):
        sent[which].append((src, dst, sem, to))
        copy_of(which, len(sent[which]) - 1).start()
        return len(sent[which]) - 1

    flushed = set()

    def flush(which, copies):
        for i in copies:
            copy_of(which, i).wait_send()
            flushed.add((which, i))

    def drain(which):
        for i in range(len(sent[which])):
            if (which, i) not in flushed:
                copy_of(which, i).wait_send()

    def arrived(dst, sem):
        pltpu.make_async_remote_copy(
            src_ref=dst, dst_ref=dst, send_sem=both_sem.at[0], recv_sem=sem,
            device_id=(partner, r), device_id_type=MESH,
        ).wait_recv()

    pl.semaphore_wait(barrier, 30)

    rings = (
        (V(um_hbm)[third], rm, 1), (V(uw_hbm)[third], rw, 1),
        (V(um_hbm)[fourth], xm, 0), (V(uw_hbm)[fourth], xw, 0), (top_hbm, tp, 1),
    )

    def spot(a, name):
        i = ids[name][rings[a][2]]
        return V(rings[a][1])[i], V(ring_sem)[a, i]

    def ring_own(which, arrays, to):
        started = []
        for a in arrays:
            dst, sem = spot(a, "own")
            started.append(send(which, rings[a][0], dst, sem, (to, r)))
        return started

    def relay(name, arrays, *to):
        for a in arrays:
            dst, sem = spot(a, name)
            arrived(at(dst), at(sem))
            for t in to:
                send(0, dst, dst, sem, (t, r))

    @pl.when(is_proc == 0)
    def _():
        ring_own(1, (0, 1), mate)
        send(1, V(um_hbm)[second], V(m2)[to_proc2], V(up_sem)[0, 2], (mate, r))
        send(1, V(uw_hbm)[second], V(w2)[to_proc2], V(up_sem)[1, 2], (mate, r))

    @pl.when(is_proc == 1)
    def _():
        ring_own(0, (0, 1, 2, 3), mate)

    send(2, V(um_hbm)[first], V(m1)[place1], V(up_sem)[2, 0], (partner, r))
    send(2, V(uw_hbm)[first], V(w1)[place1], V(up_sem)[3, 0], (partner, r))

    @pl.when(is_proc == 1)
    def _():
        send(0, V(um_hbm)[second], V(m2)[here2], V(up_sem)[0, 1], (partner, r))
        send(0, V(uw_hbm)[second], V(w2)[here2], V(up_sem)[1, 1], (partner, r))
        ring_own(0, (0, 1, 2, 3, 4), partner)

    def leaf_up(i, carry):
        for c in load(i):
            c.wait()
        solved = mul(dv[i], bv[i]).astype(BF)
        cl[i] = t_mul(solved, uv[i]).astype(BF)
        return carry

    lax.fori_loop(0, 4, leaf_up, 0)

    def node_up(pair, m, w):
        inner = mul_t(pair, m).astype(BF)
        return mul(inner, w).astype(BF)

    def node_down(pair, t, m, w):
        x = (pair.astype(F32) - mul_t(t, w)).astype(BF)
        return mul_t(x, m).astype(BF)

    def side(ref, i):
        return jnp.concatenate([ref[2 * i], ref[2 * i + 1]], axis=1)

    def local_up(i, carry):
        for c in load_local(i):
            c.wait()
        cn[i] = node_up(side(cl, i), lm[i], lw[i])
        return carry

    lax.fori_loop(0, 2, local_up, 0)
    for c in load_local(2):
        c.wait()
    ct[...] = node_up(side(cn, 0), lm[2], lw[2])

    send(2, V(ct)[pl.ds(128 - 128 * k, 128)], V(p1)[k], V(small_sem)[0], (partner, r))
    p1[k] = ct[pl.ds(pl.multiple_of(128 * k, 128), 128), :]
    for c in own:
        c.wait()
    arrived(m1.at[other1], up_sem.at[2, 0])
    arrived(w1.at[other1], up_sem.at[3, 0])
    arrived(p1.at[1 - k], small_sem.at[0])
    c1[...] = node_up(side(p1, 0), m1[...], w1[...])

    def own_gain(e):
        m1h = m1[pl.ds(pl.multiple_of(256 * k, 256), 256), :]
        e = mul(m1h, mul(w1[...], e).astype(BF)).astype(BF)
        lo = mul(lm[2], mul(lw[2], e).astype(BF)).astype(BF)
        for n in range(2):
            half = lo[256 * n : 256 * n + 256]
            e2 = mul(lm[n], mul(lw[n], half).astype(BF)).astype(BF)
            for j in range(2):
                i = 2 * n + j
                ue = mul(uv[i], e2[256 * j : 256 * j + 256, :]).astype(BF)
                hv[i] = mul(dv[i], ue).astype(BF)

    @pl.when(is_proc == 0)
    def _():
        first_sent = send(1, c1, V(p2)[side_no], V(small_sem)[1], (mate, r))
        flush(1, [first_sent])
        fourth_sent = ring_own(1, (2, 3), mate) + ring_own(1, (2, 3), far)
        flush(1, fourth_sent)
        ring_own(1, (4,), mate)
        arrived(kr, small_sem.at[10])
        own_gain(kr[...])
        arrived(f1, small_sem.at[11])

    @pl.when(is_proc == 1)
    def _():
        p2[child] = c1[...]
        relay("edge", (0, 1), mate, partner)
        ring_own(0, (2, 3), cross)
        arrived(m2.at[part2(edge2)], up_sem.at[0, 2])
        send(0, V(m2)[edge_rows2], V(m2)[edge_rows2], V(up_sem)[0, 3], (partner, r))
        arrived(w2.at[part2(edge2)], up_sem.at[1, 2])
        send(0, V(w2)[edge_rows2], V(w2)[edge_rows2], V(up_sem)[1, 3], (partner, r))
        relay("mate", (0, 1), partner)
        relay("mate", (2, 3), partner)
        for i, c in ((1, beside2), (3, beside_edge2)):
            arrived(m2.at[part2(c)], up_sem.at[0, i])
            arrived(w2.at[part2(c)], up_sem.at[1, i])
        arrived(p2.at[1 - child], small_sem.at[1])
        c2[...] = node_up(side(p2, 0), m2[...], w2[...])
        send(0, V(c2)[mate_set], V(p3)[side_no], V(small_sem)[2], (mate, r))
        p3[side_no] = c2[pl.ds(pl.multiple_of(64 * side_no, 64), 64), :]
        relay("mate_edge", (0, 1), partner)
        for a in (0, 1):
            for i in range(4):
                j = lax.rem(partner + 2 * i, 8)
                arrived(rings[a][1].at[j], ring_sem.at[a, j])
        relay("edge", (2, 3), mate, partner)
        relay("x_own", (2, 3), mate, partner)
        relay("x_edge", (2, 3), mate, partner)
        arrived(p3.at[1 - side_no], small_sem.at[2])
        m3 = rm[...].reshape(512, 512)
        w3 = rw[...].reshape(512, 256)
        pair3 = side(p3, 0)
        p4[n] = node_up(pair3, m3, w3)
        send(0, V(p4)[n], V(p4)[n], V(small_sem)[3], (opposite, r))
        ring_own(0, (4,), mate)
        relay("mate_edge", (2, 3), partner)
        relay("x_mate", (2, 3), partner)
        relay("x_mate_edge", (2, 3), partner)
        relay("edge", (4,), mate, partner)
        for a in (2, 3):
            for i in range(8):
                j = lax.rem(partner + 2 * i, 16)
                arrived(rings[a][1].at[j], ring_sem.at[a, j])
        arrived(p4.at[1 - n], small_sem.at[3])
        w4 = xw[...].reshape(512, 256)
        inner4 = mul_t(side(p4, 0), xm[...].reshape(512, 512)).astype(BF)
        root = mul(inner4, w4).astype(BF)

        @pl.when(root_home)
        def _():
            rt[eighth[0]] = root
            for i in range(15):
                send(3, V(rt)[eighth[0]], V(rt)[eighth[0]], V(root_sem)[eighth[0]], (s, plane[i]))

        t3 = jnp.where(n == 0, inner4[:, :256], inner4[:, 256:])
        t2 = node_down(pair3, t3, m3, w3)
        t2s[0] = t2[:, :256]
        t2s[1] = t2[:, 256:]
        send(0, V(t2s)[child], V(f2)[side_no], V(small_sem)[6], (mate, r))
        f2[side_no] = t2s[side_no]
        m4h = xm[pl.ds(base, 8)].reshape(256, 512)
        e = mul(m4h, w4).astype(BF)
        m3h = rm[pl.ds(4 * side_no, 4)].reshape(256, 512)
        e = mul(m3h, mul(w3, e).astype(BF)).astype(BF)
        lifted2 = mul(w2[...], e).astype(BF)
        m2_edge = m2[pl.ds(pl.multiple_of(256 - 256 * child, 256), 256), :]
        ks[...] = mul(m2_edge, lifted2).astype(BF)
        send(0, ks, kr, V(small_sem)[10], (edge, r))
        m2_own = m2[pl.ds(pl.multiple_of(256 * child, 256), 256), :]
        own_gain(mul(m2_own, lifted2).astype(BF))
        relay("mate", (4,), partner)
        relay("mate_edge", (4,), partner)
        arrived(f2.at[child], small_sem.at[6])
        t1 = node_down(side(p2, 0), f2[...].reshape(128, 256), m2[...], w2[...])
        t1s[0] = t1[:, :256]
        t1s[1] = t1[:, 256:]
        send(0, V(t1s)[side_no], f1, V(small_sem)[11], (edge, r))
        f1[...] = t1s[child]
        for i in range(4):
            j = lax.rem(partner + 2 * i, 8)
            arrived(tp.at[j], ring_sem.at[4, j])

        for i in range(1, 8):
            arrived(rt.at[eighth[i]], root_sem.at[eighth[i]])

        @pl.when(jnp.logical_not(root_home))
        def _():
            arrived(rt.at[eighth[0]], root_sem.at[eighth[0]])

        total = mul_t(rt[0], tp[0])
        for j in range(1, 8):
            total += mul_t(rt[j], tp[j])
        t4[slot] = total.astype(BF)
        for i in (4, 3, 5, 2, 6, 1, 7):
            send(0, V(t4)[slot], V(t4)[slot], V(t4_sem)[slot], (column[2 * i], r))
        send(0, V(t4)[slot], V(t4)[slot], V(t4_sem)[slot], (partner, r))

    t0 = node_down(side(p1, 0), f1[...], m1[...], w1[...])
    t0s[0] = t0[:, :256]
    t0s[1] = t0[:, 256:]
    send(2, V(t0s)[1 - k], V(f0)[k], V(small_sem)[12], (partner, r))
    f0[k] = t0s[k]
    arrived(f0.at[1 - k], small_sem.at[12])
    ta = node_down(side(cn, 0), f0[...].reshape(256, 256), lm[2], lw[2])
    for n in range(2):
        tb = node_down(side(cl, n), ta[:, 256 * n : 256 * n + 256], lm[n], lw[n])
        for j in range(2):
            i = 2 * n + j
            x = (bv[i].astype(F32) - mul_t(uv[i], tb[:, 256 * j : 256 * j + 256])).astype(BF)
            sv[i] = mul(dv[i], x)

    def pass_on(which, i):
        arrived(t4.at[i], t4_sem.at[i])
        send(which, V(t4)[i], V(t4)[i], V(t4_sem)[i], (partner, r))

    @pl.when(is_proc == 0)
    def _():
        pass_on(1, slot)

    for i in near_slots:
        pass_on(2, i)
    for i in range(4):
        j = 4 * (i // 2) + 2 - 2 * k + i % 2
        arrived(t4.at[j], t4_sem.at[j])

    top[...] = (t4[0:4].astype(F32) + t4[4:8].astype(F32)).astype(BF).reshape(256, 256)
    drain(2)

    @pl.when(is_proc == 1)
    def _():
        drain(0)

        @pl.when(root_home)
        def _():
            drain(3)

    @pl.when(is_proc == 0)
    def _():
        drain(1)


def final_kernel(sv, hv, top, out_hbm, ov, out_sem):
    def last(i):
        return pltpu.make_async_copy(ov.at[i], out_hbm.at[pl.ds(i * 256, 256)], out_sem.at[i])

    def finish(i, carry):
        rows = pl.ds(pl.multiple_of(256 * lax.rem(i, 2), 256), 256)
        ov[i] = sv[i // 2, rows, :] - mul_t(hv[i // 2, rows, :], top[...])
        last(i).start()
        return carry

    lax.fori_loop(0, 8, finish, 0)
    for i in range(8):
        last(i).wait()


def body(b, d, u, lm, lw, um, uw, top):
    flat = [
        pltpu.with_memory_space_constraint(a.reshape(a.shape[-2:]), pltpu.HBM)
        for a in (b, d, u, lm, lw, um, uw, top)
    ]
    dma = pltpu.SemaphoreType.DMA
    vm = pltpu.VMEM
    inside = pl.BlockSpec(memory_space=pltpu.VMEM)
    parts = pl.pallas_call(
        kernel,
        out_shape=(
            jax.ShapeDtypeStruct((4, 512, 256), F32), jax.ShapeDtypeStruct((4, 512, 256), BF),
            jax.ShapeDtypeStruct((256, 256), BF),
        ),
        in_specs=[pl.BlockSpec(memory_space=pltpu.HBM)] * 8,
        out_specs=(inside,) * 3,
        scratch_shapes=[
            vm((4, 512, 256), BF), vm((4, 512, 512), BF), vm((4, 512, 256), BF),
            vm((3, 512, 512), BF), vm((3, 512, 256), BF),
            vm((512, 512), BF), vm((512, 256), BF), vm((512, 512), BF), vm((512, 256), BF),
            vm((8, 64, 512), BF), vm((8, 64, 256), BF), vm((16, 32, 512), BF), vm((16, 32, 256), BF),
            vm((8, 256, 256), BF),
            vm((4, 256, 256), BF), vm((2, 256, 256), BF), vm((256, 256), BF),
            vm((2, 128, 256), BF), vm((2, 128, 256), BF), vm((128, 256), BF), vm((128, 256), BF),
            vm((2, 64, 256), BF), vm((2, 64, 256), BF), vm((8, 64, 256), BF), vm((8, 64, 256), BF),
            vm((2, 64, 256), BF), vm((2, 64, 256), BF), vm((2, 128, 256), BF), vm((128, 256), BF),
            vm((2, 128, 256), BF), vm((2, 128, 256), BF), vm((256, 256), BF), vm((256, 256), BF),
            dma((5, 4)), dma((9,)), dma((7,)), dma((61,)), dma((11,)), dma((15,)),
            dma((4, 4)), dma((5, 16)), dma((13,)), dma((8,)), dma((8,)),
        ],
        compiler_params=pltpu.CompilerParams(
            collective_id=0, has_side_effects=True, vmem_limit_bytes=24 << 20
        ),
    )(*flat)
    out = pl.pallas_call(
        final_kernel,
        out_shape=jax.ShapeDtypeStruct((2048, 256), F32),
        in_specs=[inside] * 3,
        out_specs=pl.BlockSpec(memory_space=pl.ANY),
        scratch_shapes=[vm((8, 256, 256), F32), dma((8,))],
        compiler_params=pltpu.CompilerParams(vmem_limit_bytes=16 << 20),
    )(*parts)
    return out.reshape(1, 2048, 256)


def solution(mesh):
    rows = P("root", "sub", None)
    return jax.shard_map(
        body, mesh=mesh, in_specs=(rows,) * 7 + (P("root", "sub"),), out_specs=rows, check_vma=False
    )
```
